256 devices in a mesh: paths: 32 (over x, z_lo, core), trades: 8 (over z_hi, y).
Axes of the slice: x: 4, y: 4, z: 8 (z_hi: 2, z_lo: 4; z = z_hi * 4 + z_lo), core: 2. Of those that a mesh axis runs over, the one named last changes fastest.
Arguments:
- basis: bfloat16 [32768, 512], P('paths'), may hold values from -6 to 6
- coef: bfloat16 [512, 16384], P('paths', 'trades'), may hold values from -0.25 to 0.25
- membership: int32 [16384, 512], P('trades'), may hold values from -1 to 1, as said below
- counts: int32 [512], replicated, may hold values from 1 to 63, as said below
- borrow: float32 [512], replicated, may hold values from 0.3 to 3
- lend: float32 [512], replicated, may hold values from 0.3 to 3
Outputs:
- d_basis: float32 [32768, 512], P(('paths', 'trades'))
- d_coef: float32 [512, 16384], P('paths', 'trades')
The draws below stay inside these ranges and needn't reach their ends.
Inputs may be any that keep to these rules, and one draw needn't show every extreme that they name: Each row of membership has exactly one nonzero entry, 1 or -1, and every set holds at least one trade. counts[s] is the number of nonzero entries in column s of membership; some set holds exactly one trade and some set exactly 63.
All inputs are finite; a program needn't handle non-finite values.
Results may differ from the reference program's by a relative error of at most 0.0042.
Values may be sent and summed in bfloat16 or wider, within the bound.
No kernel may reach another device: no remote copies, remote signals or barrier semaphores. Data moves between devices by JAX's collectives and lax.ppermute only.
A program may use at most 64 MiB of HBM per device.

```python
import jax
import jax.numpy as jnp
from jax import lax

K = 512
SETS = 512
P_DEV = 1024
PATHS = 32768
NTRADES = 16384
N_PATHS = 32


def assign_sets(key):
    average = NTRADES // SETS
    half_sets = SETS // 2
    spread = jax.random.randint(jax.random.fold_in(key, 11), (half_sets,), 0, average)
    spread = jnp.where(jnp.arange(half_sets, dtype=jnp.int32) == 0, average - 1, spread).astype(jnp.int32)
    sizes = jnp.concatenate([average - spread, average + spread]).astype(jnp.int32)
    which = jax.random.permutation(jax.random.fold_in(key, 12), SETS)
    set_sizes = sizes[which].astype(jnp.int32)
    ends = jnp.cumsum(set_sizes).astype(jnp.int32)
    slots = jnp.arange(NTRADES, dtype=jnp.int32)
    owner = jnp.sum((ends[None, :] <= slots[:, None]).astype(jnp.int32), axis=1).astype(jnp.int32)
    order = jax.random.permutation(jax.random.fold_in(key, 13), NTRADES)
    owner = owner[order].astype(jnp.int32)
    signs = jax.random.randint(jax.random.fold_in(key, 14), (NTRADES,), 0, 2) * 2 - 1
    return (owner, signs.astype(jnp.int32))


def draw_membership(key, part):
    owner, signs = assign_sets(key)
    hit = jnp.arange(SETS, dtype=jnp.int32)[None, :] == owner[:, None]
    return jnp.where(hit, signs[:, None], 0).astype(jnp.int32)


def draw_counts(key, part):
    owner, signs = assign_sets(key)
    hit = jnp.arange(SETS, dtype=jnp.int32)[None, :] == owner[:, None]
    return jnp.sum(hit.astype(jnp.int32), axis=0).astype(jnp.int32)


def funding_spreads(key):
    upper_bit = jax.random.randint(jax.random.fold_in(key, 21), (SETS,), 0, 2)
    first = jax.random.uniform(jax.random.fold_in(key, 22), (SETS,), jnp.float32)
    second = jax.random.uniform(jax.random.fold_in(key, 23), (SETS,), jnp.float32)
    higher = jnp.exp(jnp.log(2.0) + (jnp.log(3.0) - jnp.log(2.0)) * first)
    lower = jnp.exp(jnp.log(0.3) + (jnp.log(0.6) - jnp.log(0.3)) * second)
    borrow_side = jnp.where(upper_bit == 1, higher, lower).astype(jnp.float32)
    lend_side = jnp.where(upper_bit == 1, lower, higher).astype(jnp.float32)
    return (borrow_side, lend_side)


def draw_borrow(key, part):
    borrow_side, lend_side = funding_spreads(key)
    return borrow_side.astype(jnp.float32)


def draw_lend(key, part):
    borrow_side, lend_side = funding_spreads(key)
    return lend_side.astype(jnp.float32)


def raised(entries, rng, source, target, parts, factor):
    owner, partner = [(jnp.arange(entries.shape[axis_at]) // (entries.shape[axis_at] // parts)).reshape([-1 if axis == axis_at else 1 for axis in range(entries.ndim)]) for axis_at in (source, target)]
    chosen = jax.random.permutation(rng, parts)[partner]
    strong = (owner == chosen) | (owner == (partner + parts // 2) % parts)
    return jnp.where(strong, factor * entries, entries)


def levels(own_key, extent, pieces, smallest, high):
    factor_of = 1.0
    for dim, parts in pieces:
        draws = jax.random.uniform(jax.random.fold_in(jax.random.fold_in(own_key, 6), dim), (parts,), jnp.float32, smallest / len(pieces), high / len(pieces))
        factor_of = factor_of * jnp.repeat(jnp.exp(draws), extent[dim] // parts).reshape((-1,) + (1,) * (len(extent) - 1 - dim))
    return factor_of


def noise(rng, shape, scale, bound, pieces=(), kind=jnp.bfloat16):
    array = scale * jax.random.normal(rng, shape, jnp.float32)
    if pieces:
        array = array * levels(rng, shape, pieces, -0.22, 0.18)
    return jnp.clip(array, -bound, bound).astype(kind)


def heavy_noise(own_key, shape, scale, most, cuts, heavy, kind=jnp.bfloat16):
    result = scale * jax.random.normal(own_key, shape, jnp.float32)
    if cuts:
        result = result * levels(own_key, shape, cuts, -0.22, 0.18)
    return jnp.clip(raised(result, jax.random.fold_in(own_key, 3), *heavy), -most, most).astype(kind)


def setup_inputs(seed: int = 0) -> dict:
    seeds = jax.random.split(jax.random.key(seed), 7)
    basis = heavy_noise(seeds[0], (PATHS, K), 1.0, 6.0, ((0, 32),), (0, 1, 32, 2.75))
    coef = noise(seeds[1], (K, NTRADES), K ** -0.5, 0.25, ((0, 32), (1, 8)))
    membership = draw_membership(jax.random.fold_in(seeds[6], 71), 0)
    counts = draw_counts(jax.random.fold_in(seeds[6], 71), 0)
    borrow = draw_borrow(jax.random.fold_in(seeds[6], 71), 0)
    lend = draw_lend(jax.random.fold_in(seeds[6], 71), 0)
    return dict(basis=basis, coef=coef, membership=membership, counts=counts, borrow=borrow, lend=lend)


def reference(basis, coef, membership, counts, borrow, lend):
    high = lax.Precision.HIGHEST
    member = membership.astype(jnp.float32)
    scale = 1.0 / jnp.sqrt(counts.astype(jnp.float32))
    coef_wide = coef.astype(jnp.float32)
    blocks = basis.reshape(N_PATHS, P_DEV, K)

    def step(carry, block):
        block_wide = block.astype(jnp.float32)
        trade_value = jnp.dot(block_wide, coef_wide, precision=high)
        exposure = jax.nn.softplus(trade_value).astype(jnp.bfloat16)
        netted = jnp.dot(exposure.astype(jnp.float32), member, precision=high)
        scaled = netted * scale
        set_grad = ((borrow * jax.nn.sigmoid(scaled) + lend * jax.nn.sigmoid(-scaled)) * scale).astype(jnp.bfloat16)
        trade_grad = jnp.dot(set_grad.astype(jnp.float32), member.T, precision=high)
        value_grad = (trade_grad * jax.nn.sigmoid(trade_value)).astype(jnp.bfloat16).astype(jnp.float32)
        d_block = jnp.dot(value_grad, coef_wide.T, precision=high)
        carry = carry + jnp.dot(block_wide.T, value_grad, precision=high)
        return (carry, d_block)
    total, d_blocks = lax.scan(step, jnp.zeros((K, NTRADES), jnp.float32), blocks)
    d_coef = total * (1.0 / jnp.sqrt(jnp.float32(PATHS)))
    return (d_blocks.reshape(PATHS, K), d_coef)
```

```python
import jax
import jax.numpy as jnp
from jax import lax
from jax.sharding import Mesh, PartitionSpec as P

AXES = ("x", "zl", "core", "zh", "y")
NX, NZL, NC, NZH, NY = 4, 4, 2, 2, 4
NZ = NZL * NZH
F32 = jnp.float32
BF16 = jnp.bfloat16


def z_index(z):
    return (z % NZL) * NZH + (z // NZL) % NZH


def from_x(a, j):
    return lax.ppermute(a, "x", [((i + j) % NX, i) for i in range(NX)])


def from_y(a, j):
    return lax.ppermute(a, "y", [((i + j) % NY, i) for i in range(NY)])


def from_z(a, j):
    return lax.ppermute(
        a, ("zl", "zh"), [(z_index((i + j) % NZ), z_index(i)) for i in range(NZ)]
    )


def swap_core(a):
    return lax.ppermute(a, "core", [(0, 1), (1, 0)])


def swap_zh(a):
    return lax.ppermute(a, "zh", [(0, 1), (1, 0)])


def rotated(stack, start):
    return lax.dynamic_slice_in_dim(
        jnp.concatenate([stack, stack]), start, stack.shape[0], 0
    )


def body(basis, coef, membership, counts, borrow, lend):
    x, zl, c, zh, y = (lax.axis_index(a) for a in AXES)
    k_all, sets = basis.shape[1], membership.shape[1]
    rows = basis.shape[0] // NZH
    share = rows // NY
    k_dev = coef.shape[0]
    cols = coef.shape[1] // NC
    k_x = k_all // NX
    k_z = k_x // NZL

    my_half = lax.dynamic_slice_in_dim(coef, c * cols, cols, 1)
    to_sibling = lax.dynamic_slice_in_dim(coef, (1 - c) * cols, cols, 1)
    got = swap_core(to_sibling)
    block = jnp.where(
        c == 0, jnp.concatenate([my_half, got]), jnp.concatenate([got, my_half])
    )
    ring = [block] + [from_z(block, j) for j in range(1, NZ)]

    seg = lax.dynamic_slice_in_dim(basis, zh * rows, rows, 0).reshape(NY, share, k_all)
    mine = rotated(seg, y).reshape(rows, k_all)
    paths = jnp.concatenate([mine, swap_core(mine)])

    half = lax.dynamic_slice_in_dim(membership, c * cols, cols, 0)
    place = jnp.arange(1, sets + 1, dtype=jnp.int32)
    code = jnp.sum(half * place[None, :], axis=1)
    code = jnp.concatenate([code, swap_zh(code)])
    member = jnp.where(
        jnp.abs(code)[:, None] == place[None, :], jnp.sign(code)[:, None], 0
    ).astype(BF16)

    near, far = [], []
    for j in range(NZL):
        straight = zl + j < NZL
        near.append(jnp.where(straight, ring[j], ring[j + NZL]))
        far.append(jnp.where(straight, ring[j + NZL], ring[j]))
    layer = jnp.stack(
        [rotated(jnp.stack(near), NZL - zl), rotated(jnp.stack(far), NZL - zl)]
    )
    layers = jnp.stack([layer] + [from_x(layer, j) for j in range(1, NX)])
    layers = rotated(layers, NX - x)
    coef_full = (
        layers.transpose(0, 2, 3, 1, 4).reshape(k_all, NZH * cols)
    )

    trade_value = jnp.dot(paths, coef_full, preferred_element_type=F32)
    exposure = jax.nn.softplus(trade_value).astype(BF16)
    partial_net = jnp.dot(exposure, member, preferred_element_type=F32)
    chip_net = (partial_net[:rows] + swap_core(partial_net[rows:])).reshape(NY, share, sets)
    chip_low = chip_net.astype(BF16)
    netted = chip_net[0]
    for j in range(1, NY):
        netted = netted + from_y(chip_low[j], NY - j).astype(F32)

    scale = lax.rsqrt(counts.astype(F32))
    scaled = netted * scale
    grad = (borrow * jax.nn.sigmoid(scaled) + lend * jax.nn.sigmoid(-scaled)) * scale
    grad = grad.astype(BF16)
    grad_mine = jnp.concatenate([grad] + [from_y(grad, j) for j in range(1, NY)])
    set_grad = jnp.concatenate([grad_mine, swap_core(grad_mine)])

    trade_grad = lax.dot_general(
        set_grad, member, (((1,), (1,)), ((), ())), preferred_element_type=F32
    )
    value_grad = (trade_grad * jax.nn.sigmoid(trade_value)).astype(BF16)

    product = lax.dot_general(
        paths, value_grad, (((0,), (0,)), ((), ())), preferred_element_type=F32
    ).reshape(NX, k_x, NZH * cols)

    def part_x(j):
        return lax.dynamic_index_in_dim(product, (x + j) % NX, 0, keepdims=False)

    total = part_x(0)
    for j in range(1, NX):
        total = total + from_x(part_x(j).astype(BF16), NX - j).astype(F32)
    total = total.reshape(NZL, k_z, NZH, cols)

    def part_z(j):
        row = (zl + j) % NZL
        side = ((zl + j) // NZL) % NZH
        return lax.dynamic_slice(total, (row, 0, side, 0), (1, k_z, 1, cols)).reshape(k_z, cols)

    kept = part_z(0)
    for j in range(1, NZ):
        kept = kept + from_z(part_z(j).astype(BF16), NZ - j).astype(F32)
    kept = kept.reshape(NC, k_dev, cols)
    keep = lax.dynamic_index_in_dim(kept, c, 0, keepdims=False)
    got = swap_core(lax.dynamic_index_in_dim(kept, 1 - c, 0, keepdims=False))
    factor = 1.0 / jnp.sqrt(F32(basis.shape[0] * NX * NZL * NC))
    d_coef = jnp.where(
        c == 0, jnp.concatenate([keep, got], 1), jnp.concatenate([got, keep], 1)
    ) * factor

    d_paths = lax.dot_general(
        value_grad, coef_full, (((1,), (1,)), ((), ())), preferred_element_type=F32
    )
    chip_d = (d_paths[:rows] + swap_core(d_paths[rows:])).reshape(NY, share, k_all)
    d_low = chip_d.astype(BF16)
    d_basis = chip_d[0]
    for j in range(1, NY):
        d_basis = d_basis + from_y(d_low[j], NY - j).astype(F32)
    return (d_basis, d_coef)


def solution(mesh):
    grid = Mesh(mesh.devices.reshape(NX, NZL, NC, NZH, NY), AXES)
    paths, trades = ("x", "zl", "core"), ("zh", "y")
    placed = (P(paths, None), P(paths, trades), P(trades, None), P(), P(), P())
    return jax.shard_map(
        body,
        mesh=grid,
        in_specs=placed,
        out_specs=(P(paths + trades, None), P(paths, trades)),
        check_vma=False,
    )
```

```python
import jax
import jax.numpy as jnp
from jax import lax
from jax.sharding import Mesh, PartitionSpec as P

AXES = ("x", "zl", "core", "zh", "y")
NX, NZL, NC, NZH, NY = 4, 4, 2, 2, 4
F32 = jnp.float32
BF16 = jnp.bfloat16


def pull(a, axis, n, j):
    return lax.ppermute(a, axis, [((i + j) % n, i) for i in range(n)])


def push(a, axis, n, j):
    return pull(a, axis, n, n - j)


def dot(a, b, contract):
    return lax.dot_general(a, b, (contract, ((), ())), preferred_element_type=F32)


def column_order(x, zl, c, k_all, k_dev):
    at = jnp.arange(k_all, dtype=jnp.int32)
    inner = at % k_dev
    jz = (at // k_dev) % NZL
    jx = (at // (k_dev * NZL)) % NX
    side = at // (k_dev * NZL * NX)
    owner = (((x + jx) % NX) * NZL + (zl + jz) % NZL) * NC + (c + side) % NC
    return owner * k_dev + inner


def body(basis, coef, membership, counts, borrow, lend):
    x, zl, c, zh, y = (lax.axis_index(a) for a in AXES)
    k_all, sets = basis.shape[1], membership.shape[1]
    paths = basis.shape[0]
    share = paths // (NZH * NY)
    k_dev, trades = coef.shape
    k_half = k_all // NC

    near = jnp.concatenate([coef] + [pull(coef, "zl", NZL, j) for j in range(1, NZL)])
    own = jnp.concatenate([near] + [pull(near, "x", NX, j) for j in range(1, NX)])
    other = pull(own, "core", NC, 1)

    source = column_order(x, zl, c, k_all, k_dev)
    select = (jnp.arange(k_all, dtype=jnp.int32)[:, None] == source[None, :]).astype(BF16)
    grid = basis.reshape(NZH, NY, share, k_all)
    grid = jnp.where(zh == 0, grid, grid[::-1])
    twice = jnp.concatenate([grid, grid], 1)
    grid = lax.dynamic_slice_in_dim(twice, y, NY, 1)
    rows = grid.transpose(1, 0, 2, 3).reshape(paths, k_all)
    rows = dot(rows, select, ((1,), (0,))).astype(BF16)
    rows_own, rows_other = rows[:, :k_half], rows[:, k_half:]
    member = membership.astype(BF16)

    trade_value = dot(rows_own, own, ((1,), (0,))) + dot(rows_other, other, ((1,), (0,)))
    exposure = jax.nn.softplus(trade_value).astype(BF16)
    partial_net = dot(exposure, member, ((1,), (0,)))
    partial_net = partial_net.reshape(NY, NZH * share, sets)
    low_net = partial_net.astype(BF16)
    chip_net = partial_net[0]
    for j in range(1, NY):
        chip_net = chip_net + push(low_net[j], "y", NY, j).astype(F32)
    chip_net = chip_net.reshape(NZH, share, sets)
    low_net = chip_net.astype(BF16)
    netted = chip_net + pull(low_net, "zh", NZH, 1)[::-1].astype(F32)
    netted = netted.reshape(NZH * share, sets)

    scale = lax.rsqrt(counts.astype(F32))
    scaled = netted * scale
    grad = (borrow * jax.nn.sigmoid(scaled) + lend * jax.nn.sigmoid(-scaled)) * scale
    grad = grad.astype(BF16)
    set_grad = jnp.concatenate([grad] + [pull(grad, "y", NY, j) for j in range(1, NY)])

    trade_grad = dot(set_grad, member, ((1,), (1,)))
    value_grad = (trade_grad * jax.nn.sigmoid(trade_value)).astype(BF16)

    coef_rows = jnp.concatenate([own, other])
    coef_full = dot(select, coef_rows, ((1,), (0,))).astype(BF16)
    d_paths = dot(value_grad, coef_full, ((1,), (1,))).reshape(NY, NZH * share, k_all)
    low_d = d_paths.astype(BF16)
    chip_d = d_paths[0]
    for j in range(1, NY):
        chip_d = chip_d + push(low_d[j], "y", NY, j).astype(F32)
    chip_d = chip_d.reshape(NZH, share, k_all)
    d_basis = chip_d[0] + pull(chip_d[1].astype(BF16), "zh", NZH, 1).astype(F32)

    given = dot(rows_other, value_grad, ((0,), (0,)))
    taken = pull(given, "core", NC, 1)
    total = dot(rows_own, value_grad, ((0,), (0,))) + taken
    total = total.reshape(NX, NZL * k_dev, trades)
    low = total.astype(BF16)
    part = total[0]
    for j in range(1, NX):
        part = part + push(low[j], "x", NX, j).astype(F32)
    part = part.reshape(NZL, k_dev, trades)
    low = part.astype(BF16)
    last = part[0]
    for j in range(1, NZL):
        last = last + push(low[j], "zl", NZL, j).astype(F32)
    factor = 1.0 / jnp.sqrt(F32(paths * NX * NZL * NC))
    return (d_basis, last * factor)


def solution(mesh):
    grid = Mesh(mesh.devices.reshape(NX, NZL, NC, NZH, NY), AXES)
    paths, trades = ("x", "zl", "core"), ("zh", "y")
    placed = (P(paths, None), P(paths, trades), P(trades, None), P(), P(), P())
    return jax.shard_map(
        body,
        mesh=grid,
        in_specs=placed,
        out_specs=(P(paths + trades, None), P(paths, trades)),
        check_vma=False,
    )
```

```python
import jax
import jax.numpy as jnp
from jax import lax
from jax.sharding import Mesh, PartitionSpec as P

AXES = ("x", "zl", "core", "zh", "y")
NX, NZL, NC, NZH, NY = 4, 4, 2, 2, 4
F32 = jnp.float32
BF16 = jnp.bfloat16


def pull(a, axis, n, j):
    return lax.ppermute(a, axis, [((i + j) % n, i) for i in range(n)])


def push(a, axis, n, j):
    return pull(a, axis, n, n - j)


def dot(a, b, contract):
    return lax.dot_general(a, b, (contract, ((), ())), preferred_element_type=F32)


def column_order(x, zl, c, k_all, k_dev):
    at = jnp.arange(k_all, dtype=jnp.int32)
    inner = at % k_dev
    jz = (at // k_dev) % NZL
    jx = (at // (k_dev * NZL)) % NX
    side = at // (k_dev * NZL * NX)
    owner = (((x + jx) % NX) * NZL + (zl + jz) % NZL) * NC + (c + side) % NC
    return owner * k_dev + inner


def arranged_rows(basis, x, zl, c, zh, y, k_dev):
    paths, k_all = basis.shape
    source = column_order(x, zl, c, k_all, k_dev)
    select = (jnp.arange(k_all, dtype=jnp.int32)[:, None] == source[None, :]).astype(BF16)
    grid = basis.reshape(NZH, NY, paths // (NZH * NY), k_all)
    grid = jnp.where(zh == 0, grid, grid[::-1])
    twice = jnp.concatenate([grid, grid], 1)
    grid = lax.dynamic_slice_in_dim(twice, y, NY, 1)
    rows = grid.transpose(1, 0, 2, 3).reshape(paths, k_all)
    return dot(rows, select, ((1,), (0,))).astype(BF16), select


def body(basis, coef, membership, counts, borrow, lend):
    x, zl, c, zh, y = (lax.axis_index(a) for a in AXES)
    k_all, sets = basis.shape[1], membership.shape[1]
    paths = basis.shape[0]
    share = paths // (NZH * NY)
    k_dev, trades = coef.shape
    k_half = k_all // NC

    near = jnp.concatenate([coef] + [pull(coef, "zl", NZL, j) for j in range(1, NZL)])
    rows, select = arranged_rows(basis, x, zl, c, zh, y, coef.shape[0])
    near, rows = lax.optimization_barrier((near, rows))
    own = jnp.concatenate([near] + [pull(near, "x", NX, j) for j in range(1, NX)])
    other = pull(own, "core", NC, 1)

    rows_own, rows_other = rows[:, :k_half], rows[:, k_half:]
    member = membership.astype(BF16)

    trade_value = dot(rows_own, own, ((1,), (0,))) + dot(rows_other, other, ((1,), (0,)))
    exposure = jax.nn.softplus(trade_value).astype(BF16)
    partial_net = dot(exposure, member, ((1,), (0,)))
    partial_net = partial_net.reshape(NY, NZH * share, sets)
    low_net = partial_net.astype(BF16)
    chip_net = partial_net[0]
    for j in range(1, NY):
        chip_net = chip_net + push(low_net[j], "y", NY, j).astype(F32)
    chip_net = chip_net.reshape(NZH, share, sets)
    low_net = chip_net.astype(BF16)
    netted = chip_net + pull(low_net, "zh", NZH, 1)[::-1].astype(F32)
    netted = netted.reshape(NZH * share, sets)

    scale = lax.rsqrt(counts.astype(F32))
    scaled = netted * scale
    grad = (borrow * jax.nn.sigmoid(scaled) + lend * jax.nn.sigmoid(-scaled)) * scale
    grad = grad.astype(BF16)
    coef_full = dot(select[:, :k_half], own, ((1,), (0,)))
    coef_full = coef_full + dot(select[:, k_half:], other, ((1,), (0,)))
    grad, coef_full = lax.optimization_barrier((grad, coef_full.astype(BF16)))
    set_grad = jnp.concatenate([grad] + [pull(grad, "y", NY, j) for j in range(1, NY)])

    trade_grad = dot(set_grad, member, ((1,), (1,)))
    value_grad = (trade_grad * jax.nn.sigmoid(trade_value)).astype(BF16)

    d_paths = dot(value_grad, coef_full, ((1,), (1,))).reshape(NY, NZH * share, k_all)
    low_d = d_paths.astype(BF16)
    low_d, value_grad = lax.optimization_barrier((low_d, value_grad))
    chip_d = d_paths[0]
    for j in range(1, NY):
        chip_d = chip_d + push(low_d[j], "y", NY, j).astype(F32)
    chip_d = chip_d.reshape(NZH, share, k_all)
    d_basis = chip_d[0] + pull(chip_d[1].astype(BF16), "zh", NZH, 1).astype(F32)

    given = dot(rows_other, value_grad, ((0,), (0,)))
    taken = pull(given, "core", NC, 1)
    total = dot(rows_own, value_grad, ((0,), (0,))) + taken
    total = total.reshape(NX, NZL * k_dev, trades)
    low = total.astype(BF16)
    part = total[0]
    for j in range(1, NX):
        part = part + push(low[j], "x", NX, j).astype(F32)
    part = part.reshape(NZL, k_dev, trades)
    low = part.astype(BF16)
    last = part[0]
    for j in range(1, NZL):
        last = last + push(low[j], "zl", NZL, j).astype(F32)
    factor = 1.0 / jnp.sqrt(F32(paths * NX * NZL * NC))
    return (d_basis, last * factor)


def solution(mesh):
    grid = Mesh(mesh.devices.reshape(NX, NZL, NC, NZH, NY), AXES)
    paths, trades = ("x", "zl", "core"), ("zh", "y")
    placed = (P(paths, None), P(paths, trades), P(trades, None), P(), P(), P())
    return jax.shard_map(
        body,
        mesh=grid,
        in_specs=placed,
        out_specs=(P(paths + trades, None), P(paths, trades)),
        check_vma=False,
    )
```

```python
import jax
import jax.numpy as jnp
from jax import lax
from jax.sharding import Mesh, PartitionSpec as P

AXES = ("x", "zl", "core", "zh", "y")
NX, NZL, NC, NZH, NY = 4, 4, 2, 2, 4
F32 = jnp.float32
BF16 = jnp.bfloat16
ORDER = (1, 3, 2)


def pull(a, axis, n, j):
    return lax.ppermute(a, axis, [((i + j) % n, i) for i in range(n)])


def push(a, axis, n, j):
    return pull(a, axis, n, n - j)


def dot(a, b, contract):
    return lax.dot_general(a, b, (contract, ((), ())), preferred_element_type=F32)


def column_order(x, zl, c, k_all, k_dev):
    at = jnp.arange(k_all, dtype=jnp.int32)
    inner = at % k_dev
    jz = (at // k_dev) % NZL
    jx = (at // (k_dev * NZL)) % NX
    side = at // (k_dev * NZL * NX)
    owner = (((x + jx) % NX) * NZL + (zl + jz) % NZL) * NC + (c + side) % NC
    return owner * k_dev + inner


def arranged_rows(basis, x, zl, c, zh, y, k_dev):
    paths, k_all = basis.shape
    source = column_order(x, zl, c, k_all, k_dev)
    select = (jnp.arange(k_all, dtype=jnp.int32)[:, None] == source[None, :]).astype(BF16)
    grid = basis.reshape(NZH, NY, paths // (NZH * NY), k_all)
    grid = jnp.where(zh == 0, grid, grid[::-1])
    twice = jnp.concatenate([grid, grid], 1)
    grid = lax.dynamic_slice_in_dim(twice, y, NY, 1)
    rows = grid.transpose(1, 0, 2, 3).reshape(paths, k_all)
    return dot(rows, select, ((1,), (0,))).astype(BF16), select


def body(basis, coef, membership, counts, borrow, lend):
    x, zl, c, zh, y = (lax.axis_index(a) for a in AXES)
    k_all, sets = basis.shape[1], membership.shape[1]
    paths = basis.shape[0]
    share = paths // (NZH * NY)
    block = NZH * share
    k_dev, trades = coef.shape
    k_half = k_all // NC

    near = jnp.concatenate([coef] + [pull(coef, "zl", NZL, j) for j in range(1, NZL)])
    rows, select = arranged_rows(basis, x, zl, c, zh, y, k_dev)
    member = membership.astype(BF16)
    near, rows, member = lax.optimization_barrier((near, rows, member))
    own = jnp.concatenate([near] + [pull(near, "x", NX, j) for j in range(1, NX)])
    other = pull(own, "core", NC, 1)
    rows = rows.reshape(NY, block, k_all)
    rows_own = [rows[j, :, :k_half] for j in range(NY)]
    rows_other = [rows[j, :, k_half:] for j in range(NY)]

    begun = [
        lax.optimization_barrier(dot(rows_own[j], own, ((1,), (0,)))) for j in range(NY)
    ]
    value, net, moved = {}, {}, {}
    for j in ORDER + (0,):
        value[j] = begun[j] + dot(rows_other[j], other, ((1,), (0,)))
        exposure = jax.nn.softplus(value[j]).astype(BF16)
        net[j] = dot(exposure, member, ((1,), (0,)))
        if j:
            moved[j] = push(net[j].astype(BF16), "y", NY, j)
    chip_net = net[0]
    for j in ORDER:
        chip_net = chip_net + moved[j].astype(F32)
    chip_net = chip_net.reshape(NZH, share, sets)
    low_net = chip_net.astype(BF16)
    netted = chip_net + pull(low_net, "zh", NZH, 1)[::-1].astype(F32)
    netted = netted.reshape(block, sets)

    scale = lax.rsqrt(counts.astype(F32))
    scaled = netted * scale
    grad = (borrow * jax.nn.sigmoid(scaled) + lend * jax.nn.sigmoid(-scaled)) * scale
    grad = grad.astype(BF16)
    coef_full = dot(select[:, :k_half], own, ((1,), (0,)))
    coef_full = coef_full + dot(select[:, k_half:], other, ((1,), (0,)))
    grad, coef_full = lax.optimization_barrier((grad, coef_full.astype(BF16)))
    gathered = {j: pull(grad, "y", NY, j) for j in ORDER}
    gathered[0] = grad

    value_grad = {}
    for j in (0,) + ORDER:
        trade_grad = dot(gathered[j], member, ((1,), (1,)))
        value_grad[j] = (trade_grad * jax.nn.sigmoid(value[j])).astype(BF16)
    ready = lax.optimization_barrier(value_grad)
    d_path = {j: dot(ready[j], coef_full, ((1,), (1,))) for j in (0,) + ORDER}
    d_other = sum(dot(rows_other[j], value_grad[j], ((0,), (0,))) for j in (0,) + ORDER)
    moved = {j: push(d_path[j].astype(BF16), "y", NY, j) for j in ORDER}
    taken = pull(d_other, "core", NC, 1)
    d_own = sum(dot(rows_own[j], value_grad[j], ((0,), (0,))) for j in (0,) + ORDER)
    total = (d_own + taken).reshape(NX, NZL * k_dev, trades)

    low = total.astype(BF16)
    part = total[0]
    for j in range(1, NX):
        part = part + push(low[j], "x", NX, j).astype(F32)
    part = part.reshape(NZL, k_dev, trades)
    low = part.astype(BF16)
    chip_d = d_path[0]
    for j in ORDER:
        chip_d = chip_d + moved[j].astype(F32)
    chip_d = chip_d.reshape(NZH, share, k_all)
    d_basis = chip_d[0] + pull(chip_d[1].astype(BF16), "zh", NZH, 1).astype(F32)
    last = part[0]
    for j in range(1, NZL):
        last = last + push(low[j], "zl", NZL, j).astype(F32)
    factor = 1.0 / jnp.sqrt(F32(paths * NX * NZL * NC))
    return (d_basis, last * factor)


def solution(mesh):
    grid = Mesh(mesh.devices.reshape(NX, NZL, NC, NZH, NY), AXES)
    paths, trades = ("x", "zl", "core"), ("zh", "y")
    placed = (P(paths, None), P(paths, trades), P(trades, None), P(), P(), P())
    return jax.shard_map(
        body,
        mesh=grid,
        in_specs=placed,
        out_specs=(P(paths + trades, None), P(paths, trades)),
        check_vma=False,
    )
```

```python
import jax
import jax.numpy as jnp
from jax import lax
from jax.sharding import Mesh, PartitionSpec as P

AXES = ("x", "zl", "core", "zh", "y")
NX, NZL, NC, NZH, NY = 4, 4, 2, 2, 4
F32 = jnp.float32
BF16 = jnp.bfloat16
ORDER = (1, 3, 2)
GROUPS = ((1, 3), (2, 0))


def pull(a, axis, n, j):
    return lax.ppermute(a, axis, [((i + j) % n, i) for i in range(n)])


def push(a, axis, n, j):
    return pull(a, axis, n, n - j)


def dot(a, b, contract):
    return lax.dot_general(a, b, (contract, ((), ())), preferred_element_type=F32)


def column_order(x, zl, c, k_all, k_dev):
    at = jnp.arange(k_all, dtype=jnp.int32)
    inner = at % k_dev
    jz = (at // k_dev) % NZL
    slot = (at // (k_dev * NZL)) % NX
    jx = sum(jnp.where(slot == i + 1, j, 0) for i, j in enumerate(ORDER))
    side = at // (k_dev * NZL * NX)
    owner = (((x + jx) % NX) * NZL + (zl + jz) % NZL) * NC + (c + side) % NC
    return owner * k_dev + inner


def arranged_rows(basis, x, zl, c, zh, y, k_dev):
    paths, k_all = basis.shape
    source = column_order(x, zl, c, k_all, k_dev)
    select = (jnp.arange(k_all, dtype=jnp.int32)[:, None] == source[None, :]).astype(BF16)
    grid = basis.reshape(NZH, NY, paths // (NZH * NY), k_all)
    grid = jnp.where(zh == 0, grid, grid[::-1])
    twice = jnp.concatenate([grid, grid], 1)
    grid = lax.dynamic_slice_in_dim(twice, y, NY, 1)
    grid = grid.transpose(1, 0, 2, 3)
    rows = jnp.stack([grid[j] for j in ORDER + (0,)]).reshape(paths, k_all)
    return dot(rows, select, ((1,), (0,))).astype(BF16), select


def body(basis, coef, membership, counts, borrow, lend):
    x, zl, c, zh, y = (lax.axis_index(a) for a in AXES)
    k_all, sets = basis.shape[1], membership.shape[1]
    paths = basis.shape[0]
    share = paths // (NZH * NY)
    block = NZH * share
    k_dev, trades = coef.shape
    k_half = k_all // NC

    near = jnp.concatenate([coef] + [pull(coef, "zl", NZL, j) for j in range(1, NZL)])
    rows, select = arranged_rows(basis, x, zl, c, zh, y, k_dev)
    member = membership.astype(BF16)
    near, rows, member = lax.optimization_barrier((near, rows, member))
    fetched = {j: pull(near, "x", NX, j) for j in (1, 3, 2)}
    own = jnp.concatenate([near] + [fetched[j] for j in ORDER])
    other = pull(own, "core", NC, 1)
    begun = lax.optimization_barrier(dot(rows[:, :k_half], own, ((1,), (0,))))
    values, net, moved, at = [], {}, {}, 0
    for group in GROUPS:
        part = slice(at, at + len(group) * block)
        at = part.stop
        value = begun[part] + dot(rows[part, k_half:], other, ((1,), (0,)))
        exposure = jnp.maximum(value, 0.0) + jnp.log1p(jnp.exp(-jnp.abs(value)))
        exposure = exposure.astype(BF16)
        found = dot(exposure, member, ((1,), (0,))).reshape(len(group), block, sets)
        values.append(value)
        for i, j in enumerate(group):
            net[j] = found[i]
            if j:
                moved[j] = push(found[i].astype(BF16), "y", NY, j)
    value = jnp.concatenate(values)
    chip_net = net[0]
    for j in ORDER:
        chip_net = chip_net + moved[j].astype(F32)
    chip_net = chip_net.reshape(NZH, share, sets)
    low_net = chip_net.astype(BF16)
    netted = chip_net + pull(low_net, "zh", NZH, 1)[::-1].astype(F32)
    netted = netted.reshape(block, sets)

    scale = lax.rsqrt(counts.astype(F32))
    scaled = netted * scale
    grad = (borrow * jax.nn.sigmoid(scaled) + lend * jax.nn.sigmoid(-scaled)) * scale
    grad = grad.astype(BF16)
    coef_full = dot(select[:, :k_half], own, ((1,), (0,)))
    coef_full = coef_full + dot(select[:, k_half:], other, ((1,), (0,)))
    grad, coef_full = lax.optimization_barrier((grad, coef_full.astype(BF16)))
    fetched = {j: pull(grad, "y", NY, j) for j in (2, 3, 1)}
    gathered = jnp.concatenate([fetched[j] for j in ORDER])
    rest, mine = slice(0, paths - block), slice(paths - block, paths)

    def backward(set_grad, value):
        trade_grad = dot(set_grad, member, ((1,), (1,)))
        return (trade_grad * jax.nn.sigmoid(value)).astype(BF16)

    left = backward(grad, value[mine])
    right = backward(gathered, value[rest])
    d_mine = dot(left, coef_full, ((1,), (1,)))
    held, right = lax.optimization_barrier((right, right))
    d_rest = dot(held, coef_full, ((1,), (1,)))
    d_path = {j: d_rest[i * block : (i + 1) * block] for i, j in enumerate(ORDER)}
    d_path[0] = d_mine
    columns = slice(k_half, k_all)
    d_other = dot(rows[mine, columns], left, ((0,), (0,)))
    d_other = d_other + dot(rows[rest, columns], right, ((0,), (0,)))
    moved = {j: push(d_path[j].astype(BF16), "y", NY, j) for j in (2, 3, 1)}
    taken = pull(d_other, "core", NC, 1)
    d_own = dot(rows[mine, :k_half], left, ((0,), (0,)))
    d_own = d_own + dot(rows[rest, :k_half], right, ((0,), (0,)))
    total = (d_own + taken).reshape(NX, NZL * k_dev, trades)

    low = total.astype(BF16)
    part = total[0]
    for i, j in enumerate(ORDER):
        part = part + push(low[i + 1], "x", NX, j).astype(F32)
    part = part.reshape(NZL, k_dev, trades)
    low = part.astype(BF16)
    chip_d = d_path[0]
    for j in ORDER:
        chip_d = chip_d + moved[j].astype(F32)
    chip_d = chip_d.reshape(NZH, share, k_all)
    d_basis = chip_d[0] + pull(chip_d[1].astype(BF16), "zh", NZH, 1).astype(F32)
    last = part[0]
    for j in range(1, NZL):
        last = last + push(low[j], "zl", NZL, j).astype(F32)
    factor = 1.0 / jnp.sqrt(F32(paths * NX * NZL * NC))
    return (d_basis, last * factor)


def solution(mesh):
    grid = Mesh(mesh.devices.reshape(NX, NZL, NC, NZH, NY), AXES)
    paths, trades = ("x", "zl", "core"), ("zh", "y")
    placed = (P(paths, None), P(paths, trades), P(trades, None), P(), P(), P())
    return jax.shard_map(
        body,
        mesh=grid,
        in_specs=placed,
        out_specs=(P(paths + trades, None), P(paths, trades)),
        check_vma=False,
    )
```

```python
import jax
import jax.numpy as jnp
from jax import lax
from jax.sharding import Mesh, PartitionSpec as P

AXES = ("x", "zl", "core", "zh", "y")
NX, NZL, NC, NZH, NY = 4, 4, 2, 2, 4
F32 = jnp.float32
BF16 = jnp.bfloat16
ORDER = (1, 3, 2)
XORDER = (2, 3, 1)
GROUPS = ((1, 3), (2, 0))


def pull(a, axis, n, j):
    return lax.ppermute(a, axis, [((i + j) % n, i) for i in range(n)])


def push(a, axis, n, j):
    return pull(a, axis, n, n - j)


def dot(a, b, contract):
    return lax.dot_general(a, b, (contract, ((), ())), preferred_element_type=F32)


def column_order(x, zl, c, k_all, k_dev):
    at = jnp.arange(k_all, dtype=jnp.int32)
    inner = at % k_dev
    jz = (at // k_dev) % NZL
    slot = (at // (k_dev * NZL)) % NX
    jx = sum(jnp.where(slot == i + 1, j, 0) for i, j in enumerate(XORDER))
    side = at // (k_dev * NZL * NX)
    owner = (((x + jx) % NX) * NZL + (zl + jz) % NZL) * NC + (c + side) % NC
    return owner * k_dev + inner


def arranged_rows(basis, x, zl, c, zh, y, k_dev):
    paths, k_all = basis.shape
    source = column_order(x, zl, c, k_all, k_dev)
    select = (jnp.arange(k_all, dtype=jnp.int32)[:, None] == source[None, :]).astype(BF16)
    grid = basis.reshape(NZH, NY, paths // (NZH * NY), k_all)
    grid = jnp.where(zh == 0, grid, grid[::-1])
    twice = jnp.concatenate([grid, grid], 1)
    grid = lax.dynamic_slice_in_dim(twice, y, NY, 1)
    grid = grid.transpose(1, 0, 2, 3)
    rows = jnp.stack([grid[j] for j in ORDER + (0,)]).reshape(paths, k_all)
    return dot(rows, select, ((1,), (0,))).astype(BF16), select


def body(basis, coef, membership, counts, borrow, lend):
    x, zl, c, zh, y = (lax.axis_index(a) for a in AXES)
    k_all, sets = basis.shape[1], membership.shape[1]
    paths = basis.shape[0]
    share = paths // (NZH * NY)
    block = NZH * share
    k_dev, trades = coef.shape
    k_half = k_all // NC

    near = jnp.concatenate([coef] + [pull(coef, "zl", NZL, j) for j in range(1, NZL)])
    rows, select = arranged_rows(basis, x, zl, c, zh, y, k_dev)
    member = membership.astype(BF16)
    near, rows, member = lax.optimization_barrier((near, rows, member))
    fetched = {j: pull(near, "x", NX, j) for j in (1, 3, 2)}
    own = jnp.concatenate([near] + [fetched[j] for j in XORDER])
    other = pull(own, "core", NC, 1)
    begun = lax.optimization_barrier(dot(rows[:, :k_half], own, ((1,), (0,))))
    values, net, moved, at = [], {}, {}, 0
    for group in GROUPS:
        part = slice(at, at + len(group) * block)
        at = part.stop
        value = begun[part] + dot(rows[part, k_half:], other, ((1,), (0,)))
        exposure = jnp.maximum(value, 0.0) + jnp.log1p(jnp.exp(-jnp.abs(value)))
        exposure = exposure.astype(BF16)
        found = dot(exposure, member, ((1,), (0,))).reshape(len(group), block, sets)
        values.append(value)
        for i, j in enumerate(group):
            net[j] = found[i]
            if j:
                moved[j] = push(found[i].astype(BF16), "y", NY, j)
    value = jnp.concatenate(values)
    chip_net = net[0]
    for j in ORDER:
        chip_net = chip_net + moved[j].astype(F32)
    chip_net = chip_net.reshape(NZH, share, sets)
    low_net = chip_net.astype(BF16)
    netted = chip_net + pull(low_net, "zh", NZH, 1)[::-1].astype(F32)
    netted = netted.reshape(block, sets)

    scale = lax.rsqrt(counts.astype(F32))
    scaled = netted * scale
    grad = (borrow * jax.nn.sigmoid(scaled) + lend * jax.nn.sigmoid(-scaled)) * scale
    grad = grad.astype(BF16)
    coef_full = dot(select[:, :k_half], own, ((1,), (0,)))
    coef_full = coef_full + dot(select[:, k_half:], other, ((1,), (0,)))
    grad, coef_full = lax.optimization_barrier((grad, coef_full.astype(BF16)))
    fetched = {j: pull(grad, "y", NY, j) for j in (2, 3, 1)}
    gathered = jnp.concatenate([fetched[j] for j in ORDER])
    rest, mine = slice(0, paths - block), slice(paths - block, paths)

    def backward(set_grad, value):
        trade_grad = dot(set_grad, member, ((1,), (1,)))
        return (trade_grad * jax.nn.sigmoid(value)).astype(BF16)

    left = backward(grad, value[mine])
    right = backward(gathered, value[rest])
    d_mine = dot(left, coef_full, ((1,), (1,)))
    held, right = lax.optimization_barrier((right, right))
    d_rest = dot(held, coef_full, ((1,), (1,)))
    d_path = {j: d_rest[i * block : (i + 1) * block] for i, j in enumerate(ORDER)}
    d_path[0] = d_mine
    columns = slice(k_half, k_all)
    d_other = dot(rows[mine, columns], left, ((0,), (0,)))
    d_other = d_other + dot(rows[rest, columns], right, ((0,), (0,)))
    moved = {j: push(d_path[j].astype(BF16), "y", NY, j) for j in (2, 3, 1)}
    taken = pull(d_other, "core", NC, 1)
    d_own = dot(rows[mine, :k_half], left, ((0,), (0,)))
    d_own = d_own + dot(rows[rest, :k_half], right, ((0,), (0,)))
    total = (d_own + taken).reshape(NX, NZL * k_dev, trades)

    low = total.astype(BF16)
    part = total[0]
    for i, j in reversed(list(enumerate(XORDER))):
        part = part + push(low[i + 1], "x", NX, j).astype(F32)
    part = part.reshape(NZL, k_dev, trades)
    low = part.astype(BF16)
    chip_d = d_path[0]
    for j in ORDER:
        chip_d = chip_d + moved[j].astype(F32)
    chip_d = chip_d.reshape(NZH, share, k_all)
    d_basis = chip_d[0] + pull(chip_d[1].astype(BF16), "zh", NZH, 1).astype(F32)
    last = part[0]
    for j in range(1, NZL):
        last = last + push(low[j], "zl", NZL, j).astype(F32)
    factor = 1.0 / jnp.sqrt(F32(paths * NX * NZL * NC))
    return (d_basis, last * factor)


def solution(mesh):
    grid = Mesh(mesh.devices.reshape(NX, NZL, NC, NZH, NY), AXES)
    paths, trades = ("x", "zl", "core"), ("zh", "y")
    placed = (P(paths, None), P(paths, trades), P(trades, None), P(), P(), P())
    return jax.shard_map(
        body,
        mesh=grid,
        in_specs=placed,
        out_specs=(P(paths + trades, None), P(paths, trades)),
        check_vma=False,
    )
```

```python
import jax
import jax.numpy as jnp
from jax import lax
from jax.sharding import Mesh, PartitionSpec as P

AXES = ("x", "zl", "core", "zh", "y")
NX, NZL, NC, NZH, NY = 4, 4, 2, 2, 4
F32 = jnp.float32
BF16 = jnp.bfloat16
ORDER = (1, 3, 2)
XORDER = (2, 3, 1)
ZORDER = (1, 3, 2)
GROUPS = ((1, 3), (2, 0))


def pull(a, axis, n, j):
    return lax.ppermute(a, axis, [((i + j) % n, i) for i in range(n)])


def push(a, axis, n, j):
    return pull(a, axis, n, n - j)


def dot(a, b, contract):
    return lax.dot_general(a, b, (contract, ((), ())), preferred_element_type=F32)


def listed(slot, order):
    return sum(jnp.where(slot == i + 1, j, 0) for i, j in enumerate(order))


def column_order(x, zl, c, k_all, k_dev):
    at = jnp.arange(k_all, dtype=jnp.int32)
    inner = at % k_dev
    jz = listed((at // k_dev) % NZL, ZORDER)
    jx = listed((at // (k_dev * NZL)) % NX, XORDER)
    side = at // (k_dev * NZL * NX)
    owner = (((x + jx) % NX) * NZL + (zl + jz) % NZL) * NC + (c + side) % NC
    return owner * k_dev + inner


def arranged_rows(basis, x, zl, c, zh, y, k_dev):
    paths, k_all = basis.shape
    source = column_order(x, zl, c, k_all, k_dev)
    select = (jnp.arange(k_all, dtype=jnp.int32)[:, None] == source[None, :]).astype(BF16)
    grid = basis.reshape(NZH, NY, paths // (NZH * NY), k_all)
    grid = jnp.where(zh == 0, grid, grid[::-1])
    twice = jnp.concatenate([grid, grid], 1)
    grid = lax.dynamic_slice_in_dim(twice, y, NY, 1)
    grid = grid.transpose(1, 0, 2, 3)
    rows = jnp.stack([grid[j] for j in ORDER + (0,)]).reshape(paths, k_all)
    return dot(rows, select, ((1,), (0,))).astype(BF16), select


def body(basis, coef, membership, counts, borrow, lend):
    x, zl, c, zh, y = (lax.axis_index(a) for a in AXES)
    k_all, sets = basis.shape[1], membership.shape[1]
    paths = basis.shape[0]
    share = paths // (NZH * NY)
    block = NZH * share
    k_dev, trades = coef.shape
    k_half = k_all // NC

    near = jnp.concatenate([coef] + [pull(coef, "zl", NZL, j) for j in ZORDER])
    rows, select = arranged_rows(basis, x, zl, c, zh, y, k_dev)
    member = membership.astype(BF16)
    near, rows, member = lax.optimization_barrier((near, rows, member))
    fetched = {j: pull(near, "x", NX, j) for j in (1, 3, 2)}
    own = jnp.concatenate([near] + [fetched[j] for j in XORDER])
    other = pull(own, "core", NC, 1)
    begun = lax.optimization_barrier(dot(rows[:, :k_half], own, ((1,), (0,))))
    values, net, moved, at = [], {}, {}, 0
    for group in GROUPS:
        part = slice(at, at + len(group) * block)
        at = part.stop
        value = begun[part] + dot(rows[part, k_half:], other, ((1,), (0,)))
        exposure = jnp.maximum(value, 0.0) + jnp.log1p(jnp.exp(-jnp.abs(value)))
        exposure = exposure.astype(BF16)
        found = dot(exposure, member, ((1,), (0,))).reshape(len(group), block, sets)
        values.append(value)
        for i, j in enumerate(group):
            net[j] = found[i]
            if j:
                moved[j] = push(found[i].astype(BF16), "y", NY, j)
    value = jnp.concatenate(values)
    chip_net = net[0]
    for j in ORDER:
        chip_net = chip_net + moved[j].astype(F32)
    chip_net = chip_net.reshape(NZH, share, sets)
    low_net = chip_net.astype(BF16)
    netted = chip_net + pull(low_net, "zh", NZH, 1)[::-1].astype(F32)
    netted = netted.reshape(block, sets)

    scale = lax.rsqrt(counts.astype(F32))
    scaled = netted * scale
    grad = (borrow * jax.nn.sigmoid(scaled) + lend * jax.nn.sigmoid(-scaled)) * scale
    grad = grad.astype(BF16)
    coef_full = dot(select[:, :k_half], own, ((1,), (0,)))
    coef_full = coef_full + dot(select[:, k_half:], other, ((1,), (0,)))
    grad, coef_full = lax.optimization_barrier((grad, coef_full.astype(BF16)))
    fetched = {j: pull(grad, "y", NY, j) for j in (2, 3, 1)}
    gathered = jnp.concatenate([fetched[j] for j in ORDER])
    rest, mine = slice(0, paths - block), slice(paths - block, paths)

    def backward(set_grad, value):
        trade_grad = dot(set_grad, member, ((1,), (1,)))
        return (trade_grad * jax.nn.sigmoid(value)).astype(BF16)

    left = backward(grad, value[mine])
    right = backward(gathered, value[rest])
    d_mine = dot(left, coef_full, ((1,), (1,)))
    held, right = lax.optimization_barrier((right, right))
    d_rest = dot(held, coef_full, ((1,), (1,)))
    d_path = {j: d_rest[i * block : (i + 1) * block] for i, j in enumerate(ORDER)}
    d_path[0] = d_mine
    columns = slice(k_half, k_all)
    d_other = dot(rows[mine, columns], left, ((0,), (0,)))
    d_other = d_other + dot(rows[rest, columns], right, ((0,), (0,)))
    moved = {j: push(d_path[j].astype(BF16), "y", NY, j) for j in (2, 3, 1)}
    taken = pull(d_other, "core", NC, 1)
    d_own = dot(rows[mine, :k_half], left, ((0,), (0,)))
    d_own = d_own + dot(rows[rest, :k_half], right, ((0,), (0,)))
    total = (d_own + taken).reshape(NX, NZL * k_dev, trades)

    low = total.astype(BF16)
    part = total[0]
    for i, j in reversed(list(enumerate(XORDER))):
        part = part + push(low[i + 1], "x", NX, j).astype(F32)
    part = part.reshape(NZL, k_dev, trades)
    low = part.astype(BF16)
    chip_d = d_path[0]
    for j in ORDER:
        chip_d = chip_d + moved[j].astype(F32)
    chip_d = chip_d.reshape(NZH, share, k_all)
    d_basis = chip_d[0] + pull(chip_d[1].astype(BF16), "zh", NZH, 1).astype(F32)
    last = part[0]
    for i, j in enumerate(ZORDER):
        last = last + push(low[i + 1], "zl", NZL, j).astype(F32)
    factor = 1.0 / jnp.sqrt(F32(paths * NX * NZL * NC))
    return (d_basis, last * factor)


def solution(mesh):
    grid = Mesh(mesh.devices.reshape(NX, NZL, NC, NZH, NY), AXES)
    paths, trades = ("x", "zl", "core"), ("zh", "y")
    placed = (P(paths, None), P(paths, trades), P(trades, None), P(), P(), P())
    return jax.shard_map(
        body,
        mesh=grid,
        in_specs=placed,
        out_specs=(P(paths + trades, None), P(paths, trades)),
        check_vma=False,
    )
```

```python
import jax
import jax.numpy as jnp
from jax import lax
from jax.sharding import Mesh, PartitionSpec as P

AXES = ("x", "zl", "core", "zh", "y")
NX, NZL, NC, NZH, NY = 4, 4, 2, 2, 4
F32 = jnp.float32
BF16 = jnp.bfloat16
ORDER = (1, 3, 2)
XORDER = (2, 3, 1)
ZORDER = (1, 3, 2)
GROUPS = ((1, 3), (2, 0))


def pull(a, axis, n, j):
    return lax.ppermute(a, axis, [((i + j) % n, i) for i in range(n)])


def push(a, axis, n, j):
    return pull(a, axis, n, n - j)


def dot(a, b, contract):
    return lax.dot_general(a, b, (contract, ((), ())), preferred_element_type=F32)


def listed(slot, order):
    return sum(jnp.where(slot == i + 1, j, 0) for i, j in enumerate(order))


def column_order(x, zl, c, k_all, k_dev):
    at = jnp.arange(k_all, dtype=jnp.int32)
    inner = at % k_dev
    jz = listed((at // k_dev) % NZL, ZORDER)
    jx = listed((at // (k_dev * NZL)) % NX, XORDER)
    side = at // (k_dev * NZL * NX)
    owner = (((x + jx) % NX) * NZL + (zl + jz) % NZL) * NC + (c + side) % NC
    return owner * k_dev + inner


def arranged_rows(basis, x, zl, c, zh, y, k_dev):
    paths, k_all = basis.shape
    source = column_order(x, zl, c, k_all, k_dev)
    select = (jnp.arange(k_all, dtype=jnp.int32)[:, None] == source[None, :]).astype(BF16)
    grid = basis.reshape(NZH, NY, paths // (NZH * NY), k_all)
    grid = jnp.where(zh == 0, grid, grid[::-1])
    twice = jnp.concatenate([grid, grid], 1)
    grid = lax.dynamic_slice_in_dim(twice, y, NY, 1)
    grid = grid.transpose(1, 0, 2, 3)
    rows = jnp.stack([grid[j] for j in ORDER + (0,)]).reshape(paths, k_all)
    return dot(rows, select, ((1,), (0,))).astype(BF16), select


def body(basis, coef, membership, counts, borrow, lend):
    x, zl, c, zh, y = (lax.axis_index(a) for a in AXES)
    k_all, sets = basis.shape[1], membership.shape[1]
    paths = basis.shape[0]
    share = paths // (NZH * NY)
    block = NZH * share
    k_dev, trades = coef.shape
    k_half = k_all // NC

    near = jnp.concatenate([coef] + [pull(coef, "zl", NZL, j) for j in ZORDER])
    rows, select = arranged_rows(basis, x, zl, c, zh, y, k_dev)
    member = membership.astype(BF16)
    near, rows = lax.optimization_barrier((near, rows))
    fetched = {j: pull(near, "x", NX, j) for j in (1, 3, 2)}
    own = jnp.concatenate([near] + [fetched[j] for j in XORDER])
    own, member = lax.optimization_barrier((own, member))
    other = pull(own, "core", NC, 1)
    begun = lax.optimization_barrier(dot(rows[:, :k_half], own, ((1,), (0,))))
    values, net, moved, at = [], {}, {}, 0
    for group in GROUPS:
        part = slice(at, at + len(group) * block)
        at = part.stop
        value = begun[part] + dot(rows[part, k_half:], other, ((1,), (0,)))
        exposure = jnp.maximum(value, 0.0) + jnp.log1p(jnp.exp(-jnp.abs(value)))
        exposure = exposure.astype(BF16)
        found = dot(exposure, member, ((1,), (0,))).reshape(len(group), block, sets)
        values.append(value)
        for i, j in enumerate(group):
            net[j] = found[i]
            if j:
                moved[j] = push(found[i].astype(BF16), "y", NY, j)
    value = jnp.concatenate(values)
    chip_net = net[0]
    for j in ORDER:
        chip_net = chip_net + moved[j].astype(F32)
    chip_net = chip_net.reshape(NZH, share, sets)
    low_net = chip_net.astype(BF16)
    netted = chip_net + pull(low_net, "zh", NZH, 1)[::-1].astype(F32)
    netted = netted.reshape(block, sets)

    scale = lax.rsqrt(counts.astype(F32))
    scaled = netted * scale
    grad = (borrow * jax.nn.sigmoid(scaled) + lend * jax.nn.sigmoid(-scaled)) * scale
    grad = grad.astype(BF16)
    coef_full = dot(select[:, :k_half], own, ((1,), (0,)))
    coef_full = coef_full + dot(select[:, k_half:], other, ((1,), (0,)))
    grad, coef_full = lax.optimization_barrier((grad, coef_full.astype(BF16)))
    fetched = {j: pull(grad, "y", NY, j) for j in (2, 3, 1)}
    gathered = jnp.concatenate([fetched[j] for j in ORDER])
    rest, mine = slice(0, paths - block), slice(paths - block, paths)

    def backward(set_grad, value):
        trade_grad = dot(set_grad, member, ((1,), (1,)))
        return (trade_grad * jax.nn.sigmoid(value)).astype(BF16)

    left = backward(grad, value[mine])
    right = backward(gathered, value[rest])
    d_mine = dot(left, coef_full, ((1,), (1,)))
    held, right = lax.optimization_barrier((right, right))
    d_rest = dot(held, coef_full, ((1,), (1,)))
    d_path = {j: d_rest[i * block : (i + 1) * block] for i, j in enumerate(ORDER)}
    d_path[0] = d_mine
    columns = slice(k_half, k_all)
    d_other = dot(rows[mine, columns], left, ((0,), (0,)))
    d_other = d_other + dot(rows[rest, columns], right, ((0,), (0,)))
    moved = {j: push(d_path[j].astype(BF16), "y", NY, j) for j in (2, 3, 1)}
    taken = pull(d_other, "core", NC, 1)
    d_own = dot(rows[mine, :k_half], left, ((0,), (0,)))
    d_own = d_own + dot(rows[rest, :k_half], right, ((0,), (0,)))
    total = (d_own + taken).reshape(NX, NZL * k_dev, trades)

    low = total.astype(BF16)
    part = total[0]
    for i, j in reversed(list(enumerate(XORDER))):
        part = part + push(low[i + 1], "x", NX, j).astype(F32)
    part = part.reshape(NZL, k_dev, trades)
    low = part.astype(BF16)
    chip_d = d_path[0]
    for j in ORDER:
        chip_d = chip_d + moved[j].astype(F32)
    chip_d = chip_d.reshape(NZH, share, k_all)
    d_basis = chip_d[0] + pull(chip_d[1].astype(BF16), "zh", NZH, 1).astype(F32)
    last = part[0]
    for i, j in enumerate(ZORDER):
        last = last + push(low[i + 1], "zl", NZL, j).astype(F32)
    factor = 1.0 / jnp.sqrt(F32(paths * NX * NZL * NC))
    return (d_basis, last * factor)


def solution(mesh):
    grid = Mesh(mesh.devices.reshape(NX, NZL, NC, NZH, NY), AXES)
    paths, trades = ("x", "zl", "core"), ("zh", "y")
    placed = (P(paths, None), P(paths, trades), P(trades, None), P(), P(), P())
    return jax.shard_map(
        body,
        mesh=grid,
        in_specs=placed,
        out_specs=(P(paths + trades, None), P(paths, trades)),
        check_vma=False,
    )
```
